512 devices in a mesh: wide: 64 (over z, y), field: 8 (over x, core).
Axes of the slice: x: 4, y: 8, z: 8, core: 2. Of those that a mesh axis runs over, the one named last changes fastest.
Arguments:
- fine_field_in: bfloat16 [2048, 128, 512], P('wide', 'field'), may hold values from -6 to 6
- fine_points: float32 [4096, 3, 1024], P(('wide', 'field')), may hold values from -1 to 1
- coarse_points: float32 [4096, 3, 1024], P(('wide', 'field')), may hold values from -1 to 1
- quad_weights: float32 [4096, 1024], P(('wide', 'field')), may hold values from 0.00390625 to 0.01171875
- pair_fine: int32 [4096], P('wide'), may hold values from 0 to 31, as said below
- pair_owner: int32 [4096, 1], P('wide'), may hold values from 0 to 63; in each aligned block of 64 rows (0 to 63, 64 to 127, ...) at most 2 rows name the same one
- pair_coarse: int32 [4096], P('wide'), may hold values from 0 to 15
- coarse_faces: int32 [1024, 6], P('wide'), may hold values from 0 to 1023, as said below
- coarse_inv_mass: float32 [1024], P('wide'), may hold values from 0.5 to 2
- fine_inv_mass: float32 [2048], P('wide'), may hold values from 0.5 to 2
Outputs:
- coarse_field: bfloat16 [1024, 128, 512], P('wide', 'field')
- fine_field: bfloat16 [2048, 128, 512], P('wide', 'field')
The draws below stay inside these ranges and needn't reach their ends.
Inputs may be any that keep to these rules, and one draw needn't show every extreme that they name: `pair_fine`: within each aligned block of 64 pairs (one partition) every value 0 to 31 appears at least once. `pair_owner`: in each aligned block of 64 rows (one partition) no owner is named more than 2 times, a bound that some block reaches. `coarse_faces`: the owner of a neighbour (index // 16) differs from the element's own owner by at most one; a boundary face names the element itself.
All inputs are finite; a program needn't handle non-finite values.
Results may differ from the reference program's by a relative error of at most 0.007.
Values may be sent and summed in bfloat16 or wider, within the bound.
A program may use at most 64 MiB of HBM per device.

```python
import math
import jax
import jax.numpy as jnp
import numpy as np
from jax import lax

NB = 8
P_SIZE = 512
QUAD = 1024
CAP = 2
CE_DEV = 16
PAIRS_GRP = 64
FINE_GRP = 32
FIELDS = 128
NPAIR = 4096
NFINE = 2048
NCOARSE = 1024
N_WIDE = 64


def one_group(key):
    first, second = jax.random.split(key)
    extra = jax.random.randint(first, (PAIRS_GRP - FINE_GRP,), 0, FINE_GRP, dtype=jnp.int32)
    base = jnp.concatenate([jnp.arange(FINE_GRP, dtype=jnp.int32), extra])
    return jax.random.permutation(second, base)


def draw_pair_fine(key, part):
    keys = jax.random.split(jax.random.fold_in(key, 11), NPAIR // PAIRS_GRP)
    return jax.vmap(one_group)(keys).reshape(NPAIR).astype(jnp.int32)


def draw_coarse_faces(key, part):
    first, second, third = jax.random.split(jax.random.fold_in(key, 23), 3)
    owners = NCOARSE // CE_DEV
    own = (jnp.arange(NCOARSE, dtype=jnp.int32) // CE_DEV)[:, None]
    step = jax.random.randint(first, (NCOARSE, 6), -1, 2, dtype=jnp.int32)
    other = jnp.clip(own + step, 0, owners - 1)
    local = jax.random.randint(second, (NCOARSE, 6), 0, CE_DEV, dtype=jnp.int32)
    border = jax.random.randint(third, (NCOARSE, 6), 0, 6, dtype=jnp.int32) == 0
    itself = jnp.broadcast_to(jnp.arange(NCOARSE, dtype=jnp.int32)[:, None], (NCOARSE, 6))
    return jnp.where(border, itself, other * CE_DEV + local).astype(jnp.int32)


def touch_ends(values, key, smallest, top_value):
    extent = values.shape
    place = [jax.random.randint(jax.random.fold_in(key, axis), (), 0, extent[axis]) for axis in range(len(extent))]
    values = values.at[tuple(place)].set(smallest)
    longest = extent.index(max(extent))
    place[longest] = (place[longest] + 1) % extent[longest]
    return values.at[tuple(place)].set(top_value)


def block_levels(stream_key, dims, pieces, low, top_value):
    loudness = 1.0
    for dim, parts in pieces:
        draws = jax.random.uniform(jax.random.fold_in(jax.random.fold_in(stream_key, 6), dim), (parts,), jnp.float32, low / len(pieces), top_value / len(pieces))
        loudness = loudness * jnp.repeat(jnp.exp(draws), dims[dim] // parts).reshape((-1,) + (1,) * (len(dims) - 1 - dim))
    return loudness


def routed_block(stream_key, own, number, rows, amount, top, bound, lean):
    sequence = jax.random.permutation(stream_key, amount)
    packed, common = shares(amount, rows * top, bound, lean, True), shares(amount, rows * top, bound, lean, False)
    places = jnp.arange(amount)

    def named(lengths, rotation):
        used = int((lengths > 0).sum())
        fixed = max(1, used // 4)
        passed = fixed + (places - fixed + rotation * (used - fixed)) % max(1, amount - fixed)
        return jnp.zeros((amount,), jnp.int32).at[sequence[jnp.where(places < fixed, places, passed)]].set(jnp.asarray(lengths, jnp.int32))

    lengths = jnp.where(number % 4 == 0, named(packed, number // 4), named(common, number - number // 4 - 1))
    mixed = jax.random.permutation(jax.random.fold_in(own, 3), amount)
    donor, sink = mixed[0:amount // 2 * 2:2], mixed[1:amount // 2 * 2:2]
    slack = jnp.minimum(lengths[donor] - 1, bound - lengths[sink]) // 2
    slack = jnp.where((donor == sequence[0]) | (sink == sequence[0]) | (lengths[sink] == 0), 0, jnp.maximum(slack, 0))
    passed = jax.random.randint(jax.random.fold_in(own, 4), (amount // 2,), 0, 1 << 20) % (slack + 1)
    lengths = lengths.at[donor].add(-passed).at[sink].add(passed)
    labels = jnp.searchsorted(jnp.cumsum(lengths), jnp.arange(rows * top), side="right").astype(jnp.int32)
    listing = labels.reshape(top, rows).T
    listing = listing[jax.random.permutation(jax.random.fold_in(own, 1), rows)]
    rotation = jax.random.randint(jax.random.fold_in(own, 2), (rows, 1), 0, top)
    return jnp.take_along_axis(listing, (jnp.arange(top)[None, :] + rotation) % top, axis=1)


def shares(amount, total, limit, lean, full):
    portions = [(1 << 20) // math.isqrt(rank ** lean) + 1 for rank in range(1, amount + 1)]
    largest = limit if full else min(limit, max(-(-total // amount), total * portions[0] // sum(portions)))
    least = 1 if total - largest >= amount - 1 else 0
    holding, surplus = [largest] + [least] * (amount - 1), total - largest - least * (amount - 1)
    while surplus > 0:
        candidates = [i for i in range(1, amount) if holding[i] < largest] or [i for i in range(1, amount) if holding[i] < limit]
        mass, budget = sum([portions[i] for i in candidates]), surplus
        for i in candidates:
            more = min(limit - holding[i], max(1, budget * portions[i] // mass), surplus)
            holding[i] = holding[i] + more
            surplus = surplus - more
    return np.array(holding)


def scatter_about(key, dims, scale, most, cuts=(), held_as=jnp.bfloat16):
    level = block_levels(key, dims, cuts, -0.22, 0.18) if cuts else 1.0
    array = jax.random.normal(key, dims, jnp.float32) * scale * level
    return jnp.minimum(jnp.maximum(array, -most), most).astype(held_as)


def setup_inputs(seed: int = 0) -> dict:
    splits = jax.random.split(jax.random.key(seed), 11)
    fine_field_in = scatter_about(splits[0], (NFINE, FIELDS, P_SIZE), 1.0, 6.0, ((0, 64), (1, 8)))
    fine_points = jnp.clip(jax.random.uniform(splits[1], (NPAIR, 3, QUAD), jnp.float32, -1.0, 1.0) * block_levels(splits[1], (NPAIR, 3, QUAD), ((0, 512),), -0.4, 0.0), -1.0, 1.0)
    coarse_points = jnp.clip(jax.random.uniform(splits[2], (NPAIR, 3, QUAD), jnp.float32, -1.0, 1.0) * block_levels(splits[2], (NPAIR, 3, QUAD), ((0, 512),), -0.4, 0.0), -1.0, 1.0)
    quad_weights = jnp.clip(0.00390625 + 0.0078125 * jax.random.uniform(splits[3], (NPAIR, QUAD), jnp.float32) ** block_levels(splits[3], (NPAIR, QUAD), ((0, 512),), -0.2, 0.2), 0.00390625, 0.01171875)
    pair_fine = draw_pair_fine(jax.random.fold_in(splits[10], 71), 0)
    pair_owner_keys = jax.random.split(jax.random.fold_in(splits[5], 1), NPAIR // PAIRS_GRP)
    pair_owner_turns = jax.random.permutation(jax.random.fold_in(splits[5], 3), NPAIR // PAIRS_GRP)
    pair_owner = jax.vmap(lambda own, number: routed_block(jax.random.fold_in(splits[5], 2), own, number, PAIRS_GRP, N_WIDE, 1, CAP, 2))(pair_owner_keys, pair_owner_turns).reshape((NPAIR, 1))
    pair_coarse = touch_ends(jax.random.randint(splits[6], (NPAIR,), 0, CE_DEV), jax.random.fold_in(splits[6], 1), 0, CE_DEV - 1).astype(jnp.int32)
    coarse_faces = draw_coarse_faces(jax.random.fold_in(splits[10], 71), 0)
    coarse_inv_mass = jnp.clip(jnp.exp(math.log(2.0) - 1.3862944 * jax.random.uniform(splits[8], (NCOARSE,), jnp.float32) ** block_levels(splits[8], (NCOARSE,), ((0, 64),), -0.2, 0.2)), 0.5, 2.0)
    fine_inv_mass = jnp.clip(jnp.exp(math.log(2.0) - 1.3862944 * jax.random.uniform(splits[9], (NFINE,), jnp.float32) ** block_levels(splits[9], (NFINE,), ((0, 64),), -0.2, 0.2)), 0.5, 2.0)
    return {"fine_field_in": fine_field_in, "fine_points": fine_points, "coarse_points": coarse_points, "quad_weights": quad_weights, "pair_fine": pair_fine, "pair_owner": pair_owner, "pair_coarse": pair_coarse, "coarse_faces": coarse_faces, "coarse_inv_mass": coarse_inv_mass, "fine_inv_mass": fine_inv_mass}


DIFFUSE = 0.125

def legendre(points, count):
    values = [jnp.ones_like(points), points]
    for degree in range(1, count - 1):
        values.append(((2 * degree + 1) * points * values[degree] - degree * values[degree - 1]) / (degree + 1))
    values = values[:count]
    return jnp.stack([values[n] * math.sqrt((2 * n + 1) / 2.0) for n in range(count)])

def basis(points, count):
    table = legendre(points, count)
    product = table[:, None, None, 0, :] * table[None, :, None, 1, :] * table[None, None, :, 2, :]
    return product.reshape(count * count * count, points.shape[-1])

def build_tile(fine_pts, coarse_pts, weights):
    left = (basis(coarse_pts, NB) * weights[None, :]).astype(jnp.bfloat16)
    right = basis(fine_pts, NB).astype(jnp.bfloat16)
    return lax.dot_general(left, right, (((1,), (1,)), ((), ())), preferred_element_type=jnp.float32).astype(jnp.bfloat16)

def reference(fine_field_in, fine_points, coarse_points, quad_weights, pair_fine, pair_owner, pair_coarse, coarse_faces, coarse_inv_mass, fine_inv_mass):
    tiles = lax.map(lambda item: build_tile(item[0], item[1], item[2]), (fine_points, coarse_points, quad_weights))
    npairs = pair_fine.shape[0]
    group = (jnp.arange(npairs, dtype=jnp.int32) // PAIRS_GRP).astype(jnp.int32)
    fine_ids = (group * FINE_GRP + pair_fine).astype(jnp.int32)
    coarse_ids = (pair_owner[:, 0] * CE_DEV + pair_coarse).astype(jnp.int32)

    def add_coarse(total, item):
        tile, fine_id, coarse_id = item
        contrib = lax.dot_general(fine_field_in[fine_id], tile, (((1,), (1,)), ((), ())), preferred_element_type=jnp.float32).astype(jnp.bfloat16)
        return (total.at[coarse_id].add(contrib.astype(jnp.float32)), None)
    start = jnp.zeros((NCOARSE, FIELDS, P_SIZE), jnp.float32)
    load, _ = lax.scan(add_coarse, start, (tiles, fine_ids, coarse_ids))
    solved = coarse_inv_mass[:, None, None] * load
    beside = jnp.zeros_like(solved)
    for face in range(6):
        beside = beside + solved[coarse_faces[:, face]]
    smoothed = solved + DIFFUSE * (beside - 6.0 * solved)
    coarse_field = smoothed.astype(jnp.bfloat16)

    def add_fine(total, item):
        tile, fine_id, coarse_id = item
        term = jnp.dot(coarse_field[coarse_id], tile, preferred_element_type=jnp.float32).astype(jnp.bfloat16)
        return (total.at[fine_id].add(term.astype(jnp.float32)), None)
    start_fine = jnp.zeros((NFINE, FIELDS, P_SIZE), jnp.float32)
    fine_sum, _ = lax.scan(add_fine, start_fine, (tiles, fine_ids, coarse_ids))
    fine_field = (fine_inv_mass[:, None, None] * fine_sum).astype(jnp.bfloat16)
    return (coarse_field, fine_field)
```

```python
import math

import jax
import jax.numpy as jnp
from jax import lax
from jax.experimental import pallas as pl
from jax.experimental.pallas import tpu as pltpu
from jax.sharding import PartitionSpec as P

NB = 8
DIFFUSE = 0.125
MESH = pl.DeviceIdType.MESH
BF = jnp.bfloat16
F32 = jnp.float32
VMEM = pltpu.VMEM
LIMIT = 60 << 20

NY = 8
NW = 64
NF = 8
OFFSETS = sorted(
    [(dz, dy) for dz in range(8) for dy in range(8) if (dz, dy) != (0, 0)],
    key=lambda t: ((t[1] - t[0]) % 8, t[0]),
)


def peer(wide, offset):
    z, y = wide // NY, wide % NY
    return ((z + offset[0]) % (NW // NY)) * NY + (y + offset[1]) % NY


def iota(shape, dim):
    return lax.broadcasted_iota(jnp.int32, shape, dim)


def swap_matrix(rows, minor_out, minor_in):
    r, c = iota((rows, rows), 0), iota((rows, rows), 1)
    return (c == (r % minor_out) * minor_in + r // minor_out).astype(BF)


def dot(a, b, dims=((1,), (0,))):
    return lax.dot_general(a, b, (dims, ((), ())), preferred_element_type=F32)


def legendre_rows(x):
    scale = [math.sqrt((2 * n + 1) / 2.0) for n in range(NB)]
    rows = [jnp.full_like(x, scale[0]), x * scale[1]]
    for n in range(1, NB - 1):
        up = (2 * n + 1) / (n + 1) * scale[n + 1] / scale[n]
        down = n / (n + 1) * scale[n + 1] / scale[n - 1]
        rows.append(up * (x * rows[n]) - down * rows[n - 1])
    return rows


def basis_block(points, at, weight, out_ref, i, lanes):
    def row(d):
        return jnp.broadcast_to(points[i, d : d + 1, lanes], (NB, 128))

    first, second, third = (legendre_rows(row(at + d)) for d in range(3))
    sub = iota((NB, 128), 0)
    minor = third[0]
    for n in range(1, NB):
        minor = jnp.where(sub == n, third[n], minor)
    if weight is not None:
        minor = minor * row(weight)
    pairs = [second[b] * minor for b in range(NB)]
    for a in range(NB):
        block = jnp.concatenate([first[a] * pairs[b] for b in range(NB)], axis=0)
        out_ref[a * 64 : (a + 1) * 64, lanes] = block.astype(BF)


def project_kernel(
    pair_fine_ref,
    fine_ref,
    fine_pts_ref,
    coarse_pts_ref,
    weights_ref,
    tiles_ref,
    mixed_ref,
    picked,
    points,
    rows,
    left,
    right,
    contrib,
    swapped,
    send_sem,
    recv_sem,
):
    wide, field = lax.axis_index("wide"), lax.axis_index("field")
    barrier = pltpu.get_barrier_semaphore()
    for k in range(1, NF):
        pl.semaphore_signal(
            barrier, inc=1, device_id=(wide, (field + k) % NF), device_id_type=MESH
        )

    def pick(p, carry):
        picked[p] = fine_ref[pair_fine_ref[p]]
        return carry

    lax.fori_loop(0, 64, pick, 0)
    pl.semaphore_wait(barrier, NF - 1)
    for k in range(1, NF):
        to = (field + k) % NF
        pltpu.make_async_remote_copy(
            picked.at[pl.ds(to * 8, 8)],
            rows.at[:, pl.ds(field * 16, 16), :],
            send_sem.at[0],
            recv_sem.at[0],
            device_id=(wide, to),
            device_id_type=MESH,
        ).start()
    pltpu.make_async_copy(
        picked.at[pl.ds(field * 8, 8)], rows.at[:, pl.ds(field * 16, 16), :], recv_sem.at[0]
    ).start()

    for i in range(8):
        for d in range(3):
            points[i, d : d + 1, :] = coarse_pts_ref[d, i : i + 1, :]
            points[i, 3 + d : 4 + d, :] = fine_pts_ref[d, i : i + 1, :]
        points[i, 6:7, :] = weights_ref[i : i + 1, :]

    def build(i, carry):
        def chunk(l, c):
            lanes = pl.ds(pl.multiple_of(l * 128, 128), 128)
            basis_block(points, 0, 6, left, i, lanes)
            basis_block(points, 3, None, right, i, lanes)
            return c

        lax.fori_loop(0, 8, chunk, 0)

        def multiply(m, c):
            at = pl.ds(pl.multiple_of(m * 256, 256), 256)
            tiles_ref[i, at, :] = dot(left[at, :], right[...], ((1,), (1,))).astype(BF)
            return c

        lax.fori_loop(0, 2, multiply, 0)
        return carry

    lax.fori_loop(0, 8, build, 0)
    pltpu.make_async_copy(rows, rows, recv_sem.at[0]).wait()

    def project(i, carry):
        contrib[i] = dot(rows[i], tiles_ref[i], ((1,), (1,))).astype(BF)
        return carry

    lax.fori_loop(0, 8, project, 0)
    swap = swap_matrix(128, 8, 16)
    for k in range(NF):
        to = (field + k) % NF
        block = contrib[:, pl.ds(pl.multiple_of(to * 16, 16), 16), :].reshape(128, 512)
        swapped[k] = dot(swap, block).reshape(16, 8, 512).astype(BF)
        if k:
            pltpu.make_async_remote_copy(
                swapped.at[k],
                mixed_ref.at[:, pl.ds(field * 8, 8), :],
                send_sem.at[1],
                recv_sem.at[1],
                device_id=(wide, to),
                device_id_type=MESH,
            ).start()
        else:
            pltpu.make_async_copy(
                swapped.at[k], mixed_ref.at[:, pl.ds(field * 8, 8), :], recv_sem.at[1]
            ).start()
    for step in range(2):
        sent = swapped.at[pl.ds(0, NF - 1)]
        pltpu.make_async_copy(sent, sent, send_sem.at[step]).wait()
    pltpu.make_async_copy(mixed_ref, mixed_ref, recv_sem.at[1]).wait()


def coarse_kernel(
    meta_ref,
    mixed_ref,
    coarse_ref,
    back_ref,
    metas,
    stage,
    arrived,
    hot,
    pick,
    faces,
    inverse,
    solved,
    smooth,
    reply,
    send_sem,
    recv_sem,
):
    wide, field = lax.axis_index("wide"), lax.axis_index("field")
    row, quarter = wide // 4, wide % 4
    slab = pl.ds(pl.multiple_of(quarter * 128, 128), 128)
    barrier = pltpu.get_barrier_semaphore()
    for offset in OFFSETS:
        pl.semaphore_signal(
            barrier, inc=1, device_id=(peer(wide, offset), field), device_id_type=MESH
        )
    pl.semaphore_wait(barrier, NW - 1)

    def source(to):
        lanes = pl.ds(pl.multiple_of((to % 4) * 128, 128), 128)
        return mixed_ref.at[to // 4, :, lanes]

    def exchange(index, src, dst):
        for offset in OFFSETS:
            to = peer(wide, offset)
            pltpu.make_async_remote_copy(
                src(to),
                dst,
                send_sem.at[index],
                recv_sem.at[index],
                device_id=(to, field),
                device_id_type=MESH,
            ).start()
        pltpu.make_async_copy(src(wide), dst, recv_sem.at[index]).start()

    def wait(ref, sem):
        pltpu.make_async_copy(ref, ref, sem).wait()

    exchange(0, lambda to: meta_ref, metas.at[wide])
    exchange(1, source, arrived.at[wide])
    wait(metas, recv_sem.at[0])
    stage[...] = jnp.zeros_like(stage)
    for s in range(NW):
        stage[0, s : s + 1, :] = metas[s, :, 0:128]
        stage[1, s : s + 1, :] = metas[s, :, 128:256]
    lane128 = iota((1, 128), 1)
    element = iota((1024, 128), 0).astype(F32)

    def build_hot(k, carry):
        low, high = stage[0, pl.ds(2 * k, 1), :], stage[0, pl.ds(2 * k + 1, 1), :]
        ids = jnp.where(lane128 < 64, low, high)
        at = pl.ds(pl.multiple_of(k * 128, 128), 128)
        hot[:, at] = (element == ids).astype(F32).astype(BF)
        return carry

    lax.fori_loop(0, NW // 2, build_hot, 0)
    turned = jnp.transpose(stage[0])
    stage[0] = turned
    turned = jnp.transpose(stage[1])
    stage[1] = turned
    lane = iota((64, 128), 1)
    lane_b = iota((128, 128), 1)
    number = iota((64, 1024), 1).astype(F32)
    number_b = iota((16, 1024), 1).astype(F32)

    def build_rest(s, carry):
        ids = jnp.sum(jnp.where(lane == s, stage[0, 0:64, :], 0.0), axis=1, keepdims=True)
        at = pl.ds(pl.multiple_of(s * 64, 64), 64)
        pick[at, :] = (number == ids).astype(F32).astype(BF)
        values = jnp.sum(jnp.where(lane_b == s, stage[1], 0.0), axis=1, keepdims=True)
        count = jnp.zeros((16, 1024), F32)
        for face in range(6):
            count += (number_b == values[face * 16 : (face + 1) * 16]).astype(F32)
        at = pl.ds(pl.multiple_of(s * 16, 16), 16)
        faces[at, :] = count.astype(BF)
        inverse[at, :] = jnp.broadcast_to(values[96:112], (16, 128))
        return carry

    lax.fori_loop(0, NW, build_rest, 0)
    wait(arrived, recv_sem.at[1])

    def load_rows(m, carry):
        at = pl.ds(pl.multiple_of(m * 256, 256), 256)
        total = dot(hot[at, :], arrived[...].reshape(4096, 128)) * inverse[at, :]
        high = total.astype(BF)
        solved[at, 0:128] = high
        solved[at, 128:256] = (total - high.astype(F32)).astype(BF)
        inverse[at, :] = total
        return carry

    lax.fori_loop(0, 4, load_rows, 0)

    def smooth_rows(m, carry):
        at = pl.ds(pl.multiple_of(m * 256, 256), 256)
        both = dot(faces[at, :], solved[...])
        own = inverse[at, :]
        beside = both[:, 0:128] + both[:, 128:256]
        smooth[at, :] = (own + DIFFUSE * (beside - 6.0 * own)).astype(BF)
        return carry

    lax.fori_loop(0, 4, smooth_rows, 0)

    def gather_rows(m, carry):
        at = pl.ds(pl.multiple_of(m * 512, 512), 512)
        reply[at, :] = dot(pick[at, :], smooth[...]).astype(BF)
        return carry

    lax.fori_loop(0, 8, gather_rows, 0)
    exchange(
        2,
        lambda to: reply.at[pl.ds(pl.multiple_of(to * 64, 64), 64)],
        back_ref.at[row, :, slab],
    )
    exchange(
        3,
        lambda to: smooth.at[pl.ds(pl.multiple_of(to * 16, 16), 16)],
        coarse_ref.at[row, :, slab],
    )
    wait(back_ref, recv_sem.at[2])
    wait(coarse_ref, recv_sem.at[3])
    wait(metas.at[pl.ds(0, NW - 1)], send_sem.at[0])
    for index in (1, 2):
        wait(arrived.at[pl.ds(0, NW - 1)], send_sem.at[index])
    wait(smooth.at[pl.ds(0, 16 * (NW - 1))], send_sem.at[3])


def return_kernel(
    tiles_hbm, back_ref, terms_ref, tiles, swapped, rows, result, send_sem, recv_sem, tile_sem
):
    wide, field = lax.axis_index("wide"), lax.axis_index("field")
    load = pltpu.make_async_copy(tiles_hbm, tiles, tile_sem)
    load.start()
    barrier = pltpu.get_barrier_semaphore()
    for k in range(1, NF):
        pl.semaphore_signal(
            barrier, inc=1, device_id=(wide, (field + k) % NF), device_id_type=MESH
        )
    swap = swap_matrix(128, 16, 8)
    pl.semaphore_wait(barrier, NF - 1)
    for k in range(1, NF + 1):
        to = (field + k) % NF
        block = back_ref[:, pl.ds(pl.multiple_of(to * 8, 8), 8), :].astype(F32)
        block = block.reshape(128, 512).astype(BF)
        swapped[k - 1] = dot(swap, block).astype(BF).reshape(8, 16, 512)
        if k < NF:
            pltpu.make_async_remote_copy(
                swapped.at[k - 1],
                rows.at[:, pl.ds(field * 16, 16), :],
                send_sem.at[0],
                recv_sem.at[0],
                device_id=(wide, to),
                device_id_type=MESH,
            ).start()
        else:
            pltpu.make_async_copy(
                swapped.at[k - 1], rows.at[:, pl.ds(field * 16, 16), :], recv_sem.at[0]
            ).start()
    load.wait()
    pltpu.make_async_copy(rows, rows, recv_sem.at[0]).wait()

    def term(i, carry):
        result[i] = dot(rows[i], tiles[i]).astype(BF)
        return carry

    lax.fori_loop(0, 8, term, 0)
    for k in range(1, NF + 1):
        to = (field + k) % NF
        src = result.at[:, pl.ds(pl.multiple_of(to * 16, 16), 16), :]
        dst = terms_ref.at[pl.ds(field * 8, 8)]
        if k < NF:
            pltpu.make_async_remote_copy(
                src, dst, send_sem.at[1], recv_sem.at[1], device_id=(wide, to), device_id_type=MESH
            ).start()
        else:
            pltpu.make_async_copy(src, dst, recv_sem.at[1]).start()
    for step in range(2):
        sent = swapped.at[pl.ds(0, NF - 1)]
        pltpu.make_async_copy(sent, sent, send_sem.at[step]).wait()
    pltpu.make_async_copy(terms_ref, terms_ref, recv_sem.at[1]).wait()


def finish_kernel(
    pair_fine_ref, inverse_ref, terms_ref, coarse_ref, coarse_out_ref, fine_out_ref, total
):
    swap = swap_matrix(256, 16, 16)
    block = coarse_ref[...].reshape(256, 512)
    coarse_out_ref[...] = dot(swap, block).astype(BF).reshape(16, 16, 512)
    total[...] = jnp.zeros_like(total)

    def add(p, carry):
        e = pair_fine_ref[p]
        total[e] += terms_ref[p].astype(F32)
        return carry

    lax.fori_loop(0, 64, add, 0)

    def store(e, carry):
        fine_out_ref[e] = (inverse_ref[e] * total[e]).astype(BF)
        return carry

    lax.fori_loop(0, 32, store, 0)


def vmem():
    return pl.BlockSpec(memory_space=pltpu.VMEM)


def smem():
    return pl.BlockSpec(memory_space=pltpu.SMEM)


def anywhere():
    return pl.BlockSpec(memory_space=pl.ANY)


def call(kernel, outs, in_specs, out_specs, scratch, number=None, cost=None):
    params = {"vmem_limit_bytes": LIMIT}
    if number is not None:
        params.update(collective_id=number, has_side_effects=True)
    return pl.pallas_call(
        kernel,
        out_shape=[jax.ShapeDtypeStruct(shape, BF) for shape in outs],
        in_specs=in_specs,
        out_specs=out_specs,
        scratch_shapes=scratch,
        compiler_params=pltpu.CompilerParams(**params),
    )


def shards(
    fine_field_in,
    fine_points,
    coarse_points,
    quad_weights,
    pair_fine,
    pair_owner,
    pair_coarse,
    coarse_faces,
    coarse_inv_mass,
    fine_inv_mass,
):
    dma = pltpu.SemaphoreType.DMA
    tiles, mixed = call(
        project_kernel,
        [(8, 512, 512), (16, 64, 512)],
        [smem(), vmem(), vmem(), vmem(), vmem()],
        [vmem(), vmem()],
        [
            VMEM((64, 16, 512), BF),
            VMEM((8, 8, 1024), F32),
            VMEM((8, 128, 512), BF),
            VMEM((512, 1024), BF),
            VMEM((512, 1024), BF),
            VMEM((8, 128, 512), BF),
            VMEM((8, 16, 8, 512), BF),
            dma((2,)),
            dma((2,)),
        ],
        0,
    )(
        pair_fine,
        fine_field_in,
        jnp.transpose(fine_points, (1, 0, 2)),
        jnp.transpose(coarse_points, (1, 0, 2)),
        quad_weights,
    )
    ids = (pair_owner[:, 0] * 16 + pair_coarse).astype(F32)
    meta = jnp.concatenate(
        [
            ids,
            ids,
            coarse_faces.T.reshape(-1).astype(F32),
            coarse_inv_mass,
            jnp.zeros((16,), F32),
        ]
    ).reshape(1, 256)
    coarse, back = call(
        coarse_kernel,
        [(16, 16, 512), (16, 64, 512)],
        [vmem(), vmem()],
        [vmem(), vmem()],
        [
            VMEM((NW, 1, 256), F32),
            VMEM((2, 128, 128), F32),
            VMEM((NW, 64, 128), BF),
            VMEM((1024, 4096), BF),
            VMEM((4096, 1024), BF),
            VMEM((1024, 1024), BF),
            VMEM((1024, 128), F32),
            VMEM((1024, 256), BF),
            VMEM((1024, 128), BF),
            VMEM((4096, 128), BF),
            dma((4,)),
            dma((4,)),
        ],
        1,
    )(meta, mixed)
    (terms,) = call(
        return_kernel,
        [(64, 16, 512)],
        [anywhere(), vmem()],
        [vmem()],
        [
            VMEM((8, 512, 512), BF),
            VMEM((8, 8, 16, 512), BF),
            VMEM((8, 128, 512), BF),
            VMEM((8, 128, 512), BF),
            dma((2,)),
            dma((2,)),
            dma,
        ],
        2,
    )(tiles, back)
    return call(
        finish_kernel,
        [(16, 16, 512), (32, 16, 512)],
        [smem(), smem(), vmem(), vmem()],
        [vmem(), vmem()],
        [VMEM((32, 16, 512), F32)],
    )(pair_fine, fine_inv_mass, terms, coarse)


def solution(mesh):
    placed = (
        P("wide", "field", None),
        P(("wide", "field"), None, None),
        P(("wide", "field"), None, None),
        P(("wide", "field"), None),
        P("wide"),
        P("wide", None),
        P("wide"),
        P("wide", None),
        P("wide"),
        P("wide"),
    )
    return jax.shard_map(
        shards,
        mesh=mesh,
        in_specs=placed,
        out_specs=(P("wide", "field", None), P("wide", "field", None)),
        check_vma=False,
    )
```

```python
import math

import jax
import jax.numpy as jnp
from jax import lax
from jax.experimental import pallas as pl
from jax.experimental.pallas import tpu as pltpu
from jax.sharding import PartitionSpec as P

NB = 8
DIFFUSE = 0.125
MESH = pl.DeviceIdType.MESH
BF = jnp.bfloat16
F32 = jnp.float32
VMEM = pltpu.VMEM
LIMIT = 60 << 20

NY = 8
NW = 64
NF = 8
NC = 4


def peer(wide, k):
    z, y = wide // NY, wide % NY
    a, b = k % NY, k // NY
    return ((z + a) % (NW // NY)) * NY + (y + a + b) % NY


def iota(shape, dim):
    return lax.broadcasted_iota(jnp.int32, shape, dim)


def swap_matrix(rows, minor_out, minor_in):
    r, c = iota((rows, rows), 0), iota((rows, rows), 1)
    return (c == (r % minor_out) * minor_in + r // minor_out).astype(BF)


def dot(a, b, dims=((1,), (0,))):
    return lax.dot_general(a, b, (dims, ((), ())), preferred_element_type=F32)


def legendre_rows(x):
    scale = [math.sqrt((2 * n + 1) / 2.0) for n in range(NB)]
    rows = [jnp.full_like(x, scale[0]), x * scale[1]]
    for n in range(1, NB - 1):
        up = (2 * n + 1) / (n + 1) * scale[n + 1] / scale[n]
        down = n / (n + 1) * scale[n + 1] / scale[n - 1]
        rows.append(up * (x * rows[n]) - down * rows[n - 1])
    return rows


def basis_block(points, at, weight, out_ref, i, lanes):
    def row(d):
        return jnp.broadcast_to(points[i, d : d + 1, lanes], (NB, 128))

    first, second, third = (legendre_rows(row(at + d)) for d in range(3))
    sub = iota((NB, 128), 0)
    minor = third[0]
    for n in range(1, NB):
        minor = jnp.where(sub == n, third[n], minor)
    if weight is not None:
        minor = minor * row(weight)
    pairs = [second[b] * minor for b in range(NB)]
    for a in range(NB):
        block = jnp.concatenate([first[a] * pairs[b] for b in range(NB)], axis=0)
        out_ref[a * 64 : (a + 1) * 64, lanes] = block.astype(BF)


def remap_kernel(
    pair_fine_ref,
    owner_ref,
    pair_coarse_ref,
    coarse_faces_ref,
    coarse_inverse_ref,
    fine_ref,
    fine_pts_ref,
    coarse_pts_ref,
    weights_ref,
    coarse_ref,
    terms_ref,
    picked,
    points,
    left,
    right,
    tiles,
    rows,
    contrib,
    blocks,
    mixed,
    meta,
    metas,
    stage,
    arrived,
    hot,
    pick,
    faces,
    inverse,
    load,
    solved,
    smooth,
    reply,
    back,
    spread,
    rows_back,
    result,
    send_sem,
    rows_sem,
    blocks_sem,
    arrived_sem,
    back_sem,
    rows_back_sem,
    other_sem,
):
    wide, field = lax.axis_index("wide"), lax.axis_index("field")
    barrier = pltpu.get_barrier_semaphore()

    def greet(k, carry):
        pl.semaphore_signal(
            barrier, inc=1, device_id=(peer(wide, k), field), device_id_type=MESH
        )
        return carry

    for k in range(1, NF):
        pl.semaphore_signal(
            barrier, inc=1, device_id=(wide, (field + k) % NF), device_id_type=MESH
        )
    lax.fori_loop(1, NW, greet, 0, unroll=3)

    def wait(ref, sem):
        pltpu.make_async_copy(ref, ref, sem).wait()

    def across(index, src, dst, sem):
        def one(k, carry):
            to = peer(wide, k)
            pltpu.make_async_remote_copy(
                src(to), dst, send_sem.at[index], sem, device_id=(to, field), device_id_type=MESH
            ).start()
            return carry

        lax.fori_loop(1, NW, one, 0, unroll=3)
        pltpu.make_async_copy(src(wide), dst, sem).start()

    def along(index, src, dst, sem):
        for k in range(1, NF):
            to = (field + k) % NF
            pltpu.make_async_remote_copy(
                src(to), dst, send_sem.at[index], sem, device_id=(wide, to), device_id_type=MESH
            ).start()
        pltpu.make_async_copy(src(field), dst, sem).start()

    def pick_rows(p, carry):
        picked[p] = fine_ref[pair_fine_ref[p]]
        return carry

    lax.fori_loop(0, 64, pick_rows, 0, unroll=4)

    lane = iota((1, 128), 1)
    for c in range(NC):
        ids = jnp.zeros((1, 128), F32)
        for r in range(16):
            p = (r % 8) * 8 + 2 * c + r // 8
            number = (owner_ref[p] * 16 + pair_coarse_ref[p]).astype(F32)
            ids = jnp.where(lane % 16 == r, number, ids)
        meta[:, c * 128 : (c + 1) * 128] = ids
    values = jnp.zeros((1, 128), F32)
    for e in range(16):
        for face in range(6):
            number = coarse_faces_ref[face, e].astype(F32)
            values = jnp.where(lane == face * 16 + e, number, values)
        values = jnp.where(lane == 96 + e, coarse_inverse_ref[e], values)
    meta[:, 512:640] = values

    for i in range(8):
        for d in range(3):
            points[i, d : d + 1, :] = coarse_pts_ref[d, i : i + 1, :]
            points[i, 3 + d : 4 + d, :] = fine_pts_ref[d, i : i + 1, :]
        points[i, 6:7, :] = weights_ref[i : i + 1, :]

    def build(i, carry):
        def chunk(l, c):
            lanes = pl.ds(pl.multiple_of(l * 128, 128), 128)
            basis_block(points, 0, 6, left, i, lanes)
            basis_block(points, 3, None, right, i, lanes)
            return c

        lax.fori_loop(0, 8, chunk, 0)
        tiles[i] = dot(left[...], right[...], ((1,), (1,))).astype(BF)
        return carry

    def project(i, carry):
        contrib[i] = dot(rows[i], tiles[i], ((1,), (1,))).astype(BF)
        return carry

    def term(i, carry):
        result[i] = dot(rows_back[i], tiles[i]).astype(BF)
        return carry

    swap = swap_matrix(256, 16, 16)

    def two(c):
        return pl.ds(2 * c, 2)

    def mine(width):
        return pl.ds(pl.multiple_of(field * width, width), width)

    def block_of(to):
        return pl.ds(pl.multiple_of(to * 16, 16), 16)

    def lanes_of(to):
        return pl.ds(pl.multiple_of((to % 4) * 128, 128), 128)

    def contribute(c):
        wait(rows.at[two(c)], rows_sem.at[c])
        lax.fori_loop(2 * c, 2 * c + 2, project, 0)
        along(
            1,
            lambda to: contrib.at[two(c), block_of(to), :],
            blocks.at[two(c), field],
            blocks_sem.at[c],
        )

    def transpose(c):
        wait(blocks.at[two(c)], blocks_sem.at[c])
        mixed[c] = dot(swap, blocks[two(c)].reshape(256, 512)).astype(BF).reshape(16, 16, 512)
        across(
            2,
            lambda to: mixed.at[c, to // 4, :, lanes_of(to)],
            arrived.at[c, wide],
            arrived_sem.at[c],
        )

    lax.fori_loop(0, 2, build, 0)
    pl.semaphore_wait(barrier, NW + NF - 2)
    for c in range(NC):
        along(
            0,
            lambda to: picked.at[pl.ds(to * 8 + 2 * c, 2)],
            rows.at[two(c), mine(16), :],
            rows_sem.at[c],
        )
    across(3, lambda to: meta, metas.at[wide], other_sem.at[0])
    lax.fori_loop(2, 4, build, 0)
    contribute(0)
    lax.fori_loop(4, 6, build, 0)
    contribute(1)
    transpose(0)
    lax.fori_loop(6, 8, build, 0)
    contribute(2)
    transpose(1)
    contribute(3)
    transpose(2)
    transpose(3)

    wait(metas, other_sem.at[0])
    stage[...] = jnp.zeros_like(stage)
    for s in range(NW):
        for c in range(NC + 1):
            stage[c, s : s + 1, :] = metas[s, :, c * 128 : (c + 1) * 128]
    element = iota((1024, 128), 0).astype(F32)
    own_lanes = iota((8, 128), 1) // 16 == iota((8, 128), 0)
    for c in range(NC):

        def build_hot(k, carry):
            eight = stage[c, pl.ds(pl.multiple_of(8 * k, 8), 8), :]
            ids = jnp.sum(jnp.where(own_lanes, eight, 0.0), axis=0, keepdims=True)
            at = pl.ds(pl.multiple_of(c * 1024 + k * 128, 128), 128)
            hot[:, at] = (element == ids).astype(F32).astype(BF)
            return carry

        lax.fori_loop(0, 8, build_hot, 0)
    for c in range(NC + 1):
        turned = jnp.transpose(stage[c])
        stage[c] = turned
    few = iota((16, 128), 1)
    many = iota((128, 128), 1)
    number = iota((16, 1024), 1).astype(F32)

    def build_rest(s, carry):
        at = pl.ds(pl.multiple_of(s * 16, 16), 16)
        for c in range(NC):
            ids = jnp.sum(jnp.where(few == s, stage[c, 0:16, :], 0.0), axis=1, keepdims=True)
            pick[c, at, :] = (number == ids).astype(F32).astype(BF)
        column = jnp.sum(jnp.where(many == s, stage[NC], 0.0), axis=1, keepdims=True)
        count = jnp.zeros((16, 1024), F32)
        for face in range(6):
            count += (number == column[face * 16 : (face + 1) * 16]).astype(F32)
        faces[at, :] = count.astype(BF)
        inverse[at, :] = jnp.broadcast_to(column[96:112], (16, 128))
        return carry

    lax.fori_loop(0, NW, build_rest, 0)

    for c in range(NC):
        wait(arrived.at[c], arrived_sem.at[c])

        def load_rows(m, carry):
            at = pl.ds(pl.multiple_of(m * 256, 256), 256)
            more = dot(hot[at, c * 1024 : (c + 1) * 1024], arrived[c].reshape(1024, 128))
            if c:
                more = load[at, :] + more
            if c < NC - 1:
                load[at, :] = more
            else:
                total = more * inverse[at, :]
                high = total.astype(BF)
                solved[at, 0:128] = high
                solved[at, 128:256] = (total - high.astype(F32)).astype(BF)
                load[at, :] = total
            return carry

        lax.fori_loop(0, 4, load_rows, 0)

    def smooth_rows(m, carry):
        at = pl.ds(pl.multiple_of(m * 256, 256), 256)
        both = dot(faces[at, :], solved[...])
        own = load[at, :]
        beside = both[:, 0:128] + both[:, 128:256]
        smooth[at, :] = (own + DIFFUSE * (beside - 6.0 * own)).astype(BF)
        return carry

    lax.fori_loop(0, 4, smooth_rows, 0)

    for c in range(NC):

        def gather_rows(m, carry):
            at = pl.ds(pl.multiple_of(m * 256, 256), 256)
            out = pl.ds(pl.multiple_of(m * 16, 16), 16)
            reply[c, out] = dot(pick[c, at, :], smooth[...]).astype(BF).reshape(16, 16, 128)
            return carry

        lax.fori_loop(0, 4, gather_rows, 0)
        across(
            4,
            lambda to: reply.at[c, to],
            back.at[c, wide // 4, :, lanes_of(wide)],
            back_sem.at[c],
        )
    across(
        5,
        lambda to: smooth.at[block_of(to)],
        coarse_ref.at[wide // 4, :, lanes_of(wide)],
        other_sem.at[1],
    )

    def finish(c):
        wait(rows_back.at[two(c)], rows_back_sem.at[c])
        lax.fori_loop(2 * c, 2 * c + 2, term, 0)
        along(
            7,
            lambda to: result.at[two(c), block_of(to), :],
            terms_ref.at[pl.ds(field * 8 + 2 * c, 2)],
            other_sem.at[2],
        )

    for c in range(NC):
        wait(back.at[c], back_sem.at[c])
        turned = dot(swap, back[c].reshape(256, 512)).astype(BF)
        spread[c] = turned.reshape(2, 8, 16, 512)
        along(
            6,
            lambda to: spread.at[c, :, to],
            rows_back.at[two(c), mine(16), :],
            rows_back_sem.at[c],
        )
        if c:
            finish(c - 1)
    finish(NC - 1)
    wait(coarse_ref, other_sem.at[1])
    wait(terms_ref, other_sem.at[2])
    for index in (0, 1, 6, 7):
        wait(picked.at[pl.ds(0, 56)], send_sem.at[index])
    wait(metas.at[pl.ds(0, NW - 1)], send_sem.at[3])
    for index in (2, 4):
        for c in range(NC):
            wait(arrived.at[c, pl.ds(0, NW - 1)], send_sem.at[index])
    wait(arrived.at[0, pl.ds(0, NW - 1)], send_sem.at[5])


def finish_kernel(
    pair_fine_ref, inverse_ref, terms_ref, coarse_ref, coarse_out_ref, fine_out_ref, total
):
    swap = swap_matrix(256, 16, 16)
    block = coarse_ref[...].reshape(256, 512)
    coarse_out_ref[...] = dot(swap, block).astype(BF).reshape(16, 16, 512)
    total[...] = jnp.zeros_like(total)

    def add(p, carry):
        e = pair_fine_ref[p]
        total[e] += terms_ref[p].astype(F32)
        return carry

    lax.fori_loop(0, 64, add, 0)

    def store(e, carry):
        fine_out_ref[e] = (inverse_ref[e] * total[e]).astype(BF)
        return carry

    lax.fori_loop(0, 32, store, 0)


def vmem():
    return pl.BlockSpec(memory_space=pltpu.VMEM)


def smem():
    return pl.BlockSpec(memory_space=pltpu.SMEM)


def call(kernel, outs, in_specs, out_specs, scratch, number=None, cost=None):
    params = {"vmem_limit_bytes": LIMIT}
    if number is not None:
        params.update(collective_id=number, has_side_effects=True)
    return pl.pallas_call(
        kernel,
        out_shape=[jax.ShapeDtypeStruct(shape, BF) for shape in outs],
        in_specs=in_specs,
        out_specs=out_specs,
        scratch_shapes=scratch,
        compiler_params=pltpu.CompilerParams(**params),
    )


def shards(
    fine_field_in,
    fine_points,
    coarse_points,
    quad_weights,
    pair_fine,
    pair_owner,
    pair_coarse,
    coarse_faces,
    coarse_inv_mass,
    fine_inv_mass,
):
    dma = pltpu.SemaphoreType.DMA
    coarse, terms = call(
        remap_kernel,
        [(16, 16, 512), (64, 16, 512)],
        [smem()] * 5 + [vmem()] * 4,
        [vmem(), vmem()],
        [
            VMEM((64, 16, 512), BF),
            VMEM((8, 8, 1024), F32),
            VMEM((512, 1024), BF),
            VMEM((512, 1024), BF),
            VMEM((8, 512, 512), BF),
            VMEM((8, 128, 512), BF),
            VMEM((8, 128, 512), BF),
            VMEM((8, 8, 16, 512), BF),
            VMEM((NC, 16, 16, 512), BF),
            VMEM((1, 640), F32),
            VMEM((NW, 1, 640), F32),
            VMEM((NC + 1, 128, 128), F32),
            VMEM((NC, NW, 16, 128), BF),
            VMEM((1024, 4096), BF),
            VMEM((NC, 1024, 1024), BF),
            VMEM((1024, 1024), BF),
            VMEM((1024, 128), F32),
            VMEM((1024, 128), F32),
            VMEM((1024, 256), BF),
            VMEM((1024, 128), BF),
            VMEM((NC, NW, 16, 128), BF),
            VMEM((NC, 16, 16, 512), BF),
            VMEM((NC, 2, 8, 16, 512), BF),
            VMEM((8, 128, 512), BF),
            VMEM((8, 128, 512), BF),
            dma((8,)),
            dma((NC,)),
            dma((NC,)),
            dma((NC,)),
            dma((NC,)),
            dma((NC,)),
            dma((3,)),
        ],
        0,
    )(
        pair_fine,
        pair_owner.reshape(64),
        pair_coarse,
        coarse_faces.T,
        coarse_inv_mass,
        fine_field_in,
        jnp.transpose(fine_points, (1, 0, 2)),
        jnp.transpose(coarse_points, (1, 0, 2)),
        quad_weights,
    )
    return call(
        finish_kernel,
        [(16, 16, 512), (32, 16, 512)],
        [smem(), smem(), vmem(), vmem()],
        [vmem(), vmem()],
        [VMEM((32, 16, 512), F32)],
    )(pair_fine, fine_inv_mass, terms, coarse)


def solution(mesh):
    placed = (
        P("wide", "field", None),
        P(("wide", "field"), None, None),
        P(("wide", "field"), None, None),
        P(("wide", "field"), None),
        P("wide"),
        P("wide", None),
        P("wide"),
        P("wide", None),
        P("wide"),
        P("wide"),
    )
    return jax.shard_map(
        shards,
        mesh=mesh,
        in_specs=placed,
        out_specs=(P("wide", "field", None), P("wide", "field", None)),
        check_vma=False,
    )
```

```python
import math

import jax
import jax.numpy as jnp
from jax import lax
from jax.experimental import pallas as pl
from jax.experimental.pallas import tpu as pltpu
from jax.sharding import PartitionSpec as P

NB = 8
DIFFUSE = 0.125
MESH = pl.DeviceIdType.MESH
BF = jnp.bfloat16
F32 = jnp.float32
VMEM = pltpu.VMEM
LIMIT = 60 << 20

NY = 8
NW = 64
NF = 8
NC = 4


def peer(wide, k):
    z, y = lax.div(wide, NY), lax.rem(wide, NY)
    return lax.rem(z + k % NY, NW // NY) * NY + lax.rem(y + k % NY + k // NY, NY)


def iota(shape, dim):
    return lax.broadcasted_iota(jnp.int32, shape, dim)


def swap_matrix(rows, minor_out, minor_in):
    r, c = iota((rows, rows), 0), iota((rows, rows), 1)
    return (c == (r % minor_out) * minor_in + r // minor_out).astype(BF)


def dot(a, b, dims=((1,), (0,))):
    return lax.dot_general(a, b, (dims, ((), ())), preferred_element_type=F32)


def legendre_rows(x):
    scale = [math.sqrt((2 * n + 1) / 2.0) for n in range(NB)]
    rows = [jnp.full_like(x, scale[0]), x * scale[1]]
    for n in range(1, NB - 1):
        up = (2 * n + 1) / (n + 1) * scale[n + 1] / scale[n]
        down = n / (n + 1) * scale[n + 1] / scale[n - 1]
        rows.append(up * (x * rows[n]) - down * rows[n - 1])
    return rows


def basis_block(points, at, weight, out_ref, i, lanes):
    def row(d):
        return jnp.broadcast_to(points[i, d : d + 1, lanes], (NB, 128))

    first, second, third = (legendre_rows(row(at + d)) for d in range(3))
    sub = iota((NB, 128), 0)
    minor = third[0]
    for n in range(1, NB):
        minor = jnp.where(sub == n, third[n], minor)
    if weight is not None:
        minor = minor * row(weight)
    pairs = [second[b] * minor for b in range(NB)]
    for a in range(NB):
        block = jnp.concatenate([first[a] * pairs[b] for b in range(NB)], axis=0)
        out_ref[a * 64 : (a + 1) * 64, lanes] = block.astype(BF)


def remap_kernel(
    pair_fine_ref,
    owner_ref,
    pair_coarse_ref,
    coarse_faces_ref,
    coarse_inverse_ref,
    fine_hbm,
    fine_pts_hbm,
    coarse_pts_hbm,
    weights_hbm,
    coarse_ref,
    terms_ref,
    fine_ref,
    fine_pts_ref,
    coarse_pts_ref,
    weights_ref,
    picked,
    points,
    left,
    right,
    tiles,
    rows,
    contrib,
    blocks,
    mixed,
    meta,
    metas,
    stage,
    arrived,
    hot,
    pick,
    faces,
    inverse,
    load,
    solved,
    smooth,
    reply,
    back,
    spread,
    rows_back,
    result,
    send_sem,
    rows_sem,
    blocks_sem,
    arrived_sem,
    back_sem,
    rows_back_sem,
    other_sem,
    input_sem,
):
    wide, field = lax.axis_index("wide"), lax.axis_index("field")
    barrier = pltpu.get_barrier_semaphore()

    for k in range(1, NF):
        pl.semaphore_signal(
            barrier, inc=1, device_id=(wide, lax.rem(field + k, NF)), device_id_type=MESH
        )
    for k in range(1, NW):
        pl.semaphore_signal(
            barrier, inc=1, device_id=(peer(wide, k), field), device_id_type=MESH
        )
    inputs = [
        pltpu.make_async_copy(src, dst, input_sem.at[n])
        for n, (src, dst) in enumerate(
            (
                (fine_hbm, fine_ref),
                (coarse_pts_hbm, coarse_pts_ref),
                (fine_pts_hbm, fine_pts_ref),
                (weights_hbm, weights_ref),
            )
        )
    ]
    for copy in inputs:
        copy.start()

    def wait(ref, sem):
        pltpu.make_async_copy(ref, ref, sem).wait()

    def across(index, src, dst, sem):
        for k in range(1, NW):
            to = peer(wide, k)
            pltpu.make_async_remote_copy(
                src(to), dst, send_sem.at[index], sem, device_id=(to, field), device_id_type=MESH
            ).start()
        pltpu.make_async_copy(src(wide), dst, sem).start()

    def along(index, src, dst, sem):
        for k in range(1, NF):
            to = lax.rem(field + k, NF)
            pltpu.make_async_remote_copy(
                src(to), dst, send_sem.at[index], sem, device_id=(wide, to), device_id_type=MESH
            ).start()
        pltpu.make_async_copy(src(field), dst, sem).start()

    def two(c):
        return pl.ds(2 * c, 2)

    def mine(width):
        return pl.ds(pl.multiple_of(field * width, width), width)

    def block_of(to):
        return pl.ds(pl.multiple_of(to * 16, 16), 16)

    def lanes_of(to):
        return pl.ds(pl.multiple_of(lax.rem(to, 4) * 128, 128), 128)

    def pick_rows(p, carry):
        picked[p] = fine_ref[pair_fine_ref[p]]
        return carry

    inputs[0].wait()
    lax.fori_loop(0, 64, pick_rows, 0, unroll=8)
    pl.semaphore_wait(barrier, NW + NF - 2)

    def send_rows(c):
        along(
            0,
            lambda to: picked.at[pl.ds(to * 8 + 2 * c, 2)],
            rows.at[two(c), mine(16), :],
            rows_sem.at[c],
        )

    send_rows(0)
    send_rows(1)

    lane = iota((1, 128), 1)
    for c in range(NC):
        ids = jnp.zeros((1, 128), F32)
        for r in range(16):
            p = (r % 8) * 8 + 2 * c + r // 8
            number = (owner_ref[p] * 16 + pair_coarse_ref[p]).astype(F32)
            ids = jnp.where(lane % 16 == r, number, ids)
        meta[:, c * 128 : (c + 1) * 128] = ids
    values = jnp.zeros((1, 128), F32)
    for e in range(16):
        for face in range(6):
            number = coarse_faces_ref[face, e].astype(F32)
            values = jnp.where(lane == face * 16 + e, number, values)
        values = jnp.where(lane == 96 + e, coarse_inverse_ref[e], values)
    meta[:, 512:640] = values
    across(3, lambda to: meta, metas.at[wide], other_sem.at[0])

    for copy in inputs[1:]:
        copy.wait()
    for i in range(8):
        for d in range(3):
            points[i, d : d + 1, :] = coarse_pts_ref[d, i : i + 1, :]
            points[i, 3 + d : 4 + d, :] = fine_pts_ref[d, i : i + 1, :]
        points[i, 6:7, :] = weights_ref[i : i + 1, :]

    def build(i, carry):
        def chunk(l, c):
            lanes = pl.ds(pl.multiple_of(l * 128, 128), 128)
            basis_block(points, 0, 6, left, i, lanes)
            basis_block(points, 3, None, right, i, lanes)
            return c

        lax.fori_loop(0, 8, chunk, 0)
        tiles[i] = dot(left[...], right[...], ((1,), (1,))).astype(BF)
        return carry

    def project(i, carry):
        contrib[i] = dot(rows[i], tiles[i], ((1,), (1,))).astype(BF)
        return carry

    def term(i, carry):
        result[i] = dot(rows_back[i], tiles[i]).astype(BF)
        return carry

    swap = swap_matrix(256, 16, 16)

    def contribute(c):
        wait(rows.at[two(c)], rows_sem.at[c])
        lax.fori_loop(2 * c, 2 * c + 2, project, 0)
        along(
            1,
            lambda to: contrib.at[two(c), block_of(to), :],
            blocks.at[two(c), field],
            blocks_sem.at[c],
        )

    def transpose(c):
        wait(blocks.at[two(c)], blocks_sem.at[c])
        mixed[c] = dot(swap, blocks[two(c)].reshape(256, 512)).astype(BF).reshape(16, 16, 512)
        across(
            2,
            lambda to: mixed.at[c, lax.div(to, 4), :, lanes_of(to)],
            arrived.at[c, wide],
            arrived_sem.at[c],
        )

    lax.fori_loop(0, 2, build, 0)
    contribute(0)
    send_rows(2)
    lax.fori_loop(2, 4, build, 0)
    contribute(1)
    send_rows(3)
    transpose(0)
    lax.fori_loop(4, 6, build, 0)
    contribute(2)
    transpose(1)
    lax.fori_loop(6, 8, build, 0)
    contribute(3)
    transpose(2)
    transpose(3)

    wait(metas, other_sem.at[0])
    stage[...] = jnp.zeros_like(stage)
    for s in range(NW):
        for c in range(NC + 1):
            stage[c, s : s + 1, :] = metas[s, :, c * 128 : (c + 1) * 128]
    element = iota((1024, 128), 0).astype(F32)
    own_lanes = iota((8, 128), 1) // 16 == iota((8, 128), 0)
    for c in range(NC):

        def build_hot(k, carry):
            eight = stage[c, pl.ds(pl.multiple_of(8 * k, 8), 8), :]
            ids = jnp.sum(jnp.where(own_lanes, eight, 0.0), axis=0, keepdims=True)
            at = pl.ds(pl.multiple_of(c * 1024 + k * 128, 128), 128)
            hot[:, at] = (element == ids).astype(F32).astype(BF)
            return carry

        lax.fori_loop(0, 8, build_hot, 0)
    for c in range(NC + 1):
        turned = jnp.transpose(stage[c])
        stage[c] = turned
    few = iota((16, 128), 1)
    many = iota((128, 128), 1)
    number = iota((16, 1024), 1).astype(F32)

    def build_rest(s, carry):
        at = pl.ds(pl.multiple_of(s * 16, 16), 16)
        for c in range(NC):
            ids = jnp.sum(jnp.where(few == s, stage[c, 0:16, :], 0.0), axis=1, keepdims=True)
            pick[c, at, :] = (number == ids).astype(F32).astype(BF)
        column = jnp.sum(jnp.where(many == s, stage[NC], 0.0), axis=1, keepdims=True)
        count = jnp.zeros((16, 1024), F32)
        for face in range(6):
            count += (number == column[face * 16 : (face + 1) * 16]).astype(F32)
        faces[at, :] = count.astype(BF)
        inverse[at, :] = jnp.broadcast_to(column[96:112], (16, 128))
        return carry

    lax.fori_loop(0, NW, build_rest, 0)

    for c in range(NC):
        wait(arrived.at[c], arrived_sem.at[c])

        more = dot(hot[:, c * 1024 : (c + 1) * 1024], arrived[c].reshape(1024, 128))
        if c:
            more = load[...] + more
        if c < NC - 1:
            load[...] = more
        else:
            total = more * inverse[...]
            high = total.astype(BF)
            solved[:, 0:128] = high
            solved[:, 128:256] = (total - high.astype(F32)).astype(BF)
            load[...] = total

    def smooth_rows(m, carry):
        at = pl.ds(pl.multiple_of(m * 512, 512), 512)
        both = dot(faces[at, :], solved[...])
        own = load[at, :]
        beside = both[:, 0:128] + both[:, 128:256]
        smooth[at, :] = (own + DIFFUSE * (beside - 6.0 * own)).astype(BF)
        return carry

    lax.fori_loop(0, 2, smooth_rows, 0)

    for c in range(NC):
        reply[c] = dot(pick[c], smooth[...]).astype(BF).reshape(NW, 16, 128)
        across(
            4,
            lambda to: reply.at[c, to],
            back.at[c, lax.div(wide, 4), :, lanes_of(wide)],
            back_sem.at[c],
        )
    across(
        5,
        lambda to: smooth.at[block_of(to)],
        coarse_ref.at[lax.div(wide, 4), :, lanes_of(wide)],
        other_sem.at[1],
    )

    def finish(c):
        wait(rows_back.at[two(c)], rows_back_sem.at[c])
        lax.fori_loop(2 * c, 2 * c + 2, term, 0)
        along(
            7,
            lambda to: result.at[two(c), block_of(to), :],
            terms_ref.at[pl.ds(field * 8 + 2 * c, 2)],
            other_sem.at[2],
        )

    for c in range(NC):
        wait(back.at[c], back_sem.at[c])
        turned = dot(swap, back[c].reshape(256, 512)).astype(BF)
        spread[c] = turned.reshape(2, 8, 16, 512)
        along(
            6,
            lambda to: spread.at[c, :, to],
            rows_back.at[two(c), mine(16), :],
            rows_back_sem.at[c],
        )
        if c:
            finish(c - 1)
    finish(NC - 1)
    wait(coarse_ref, other_sem.at[1])
    wait(terms_ref, other_sem.at[2])
    for index in (0, 1, 6, 7):
        wait(picked.at[pl.ds(0, 56)], send_sem.at[index])
    wait(metas.at[pl.ds(0, NW - 1)], send_sem.at[3])
    for index in (2, 4):
        for c in range(NC):
            wait(arrived.at[c, pl.ds(0, NW - 1)], send_sem.at[index])
    wait(arrived.at[0, pl.ds(0, NW - 1)], send_sem.at[5])


def finish_kernel(
    pair_fine_ref, inverse_ref, terms_ref, coarse_ref, coarse_out_ref, fine_out_ref, total
):
    swap = swap_matrix(256, 16, 16)
    block = coarse_ref[...].reshape(256, 512)
    coarse_out_ref[...] = dot(swap, block).astype(BF).reshape(16, 16, 512)
    total[...] = jnp.zeros_like(total)

    def add(p, carry):
        e = pair_fine_ref[p]
        total[e] += terms_ref[p].astype(F32)
        return carry

    lax.fori_loop(0, 64, add, 0)

    def store(e, carry):
        fine_out_ref[e] = (inverse_ref[e] * total[e]).astype(BF)
        return carry

    lax.fori_loop(0, 32, store, 0)


def vmem():
    return pl.BlockSpec(memory_space=pltpu.VMEM)


def smem():
    return pl.BlockSpec(memory_space=pltpu.SMEM)


def anywhere():
    return pl.BlockSpec(memory_space=pl.ANY)


def call(kernel, outs, in_specs, out_specs, scratch, number=None, cost=None):
    params = {"vmem_limit_bytes": LIMIT}
    if number is not None:
        params.update(collective_id=number, has_side_effects=True)
    return pl.pallas_call(
        kernel,
        out_shape=[jax.ShapeDtypeStruct(shape, BF) for shape in outs],
        in_specs=in_specs,
        out_specs=out_specs,
        scratch_shapes=scratch,
        compiler_params=pltpu.CompilerParams(**params),
    )


def shards(
    fine_field_in,
    fine_points,
    coarse_points,
    quad_weights,
    pair_fine,
    pair_owner,
    pair_coarse,
    coarse_faces,
    coarse_inv_mass,
    fine_inv_mass,
):
    dma = pltpu.SemaphoreType.DMA
    coarse, terms = call(
        remap_kernel,
        [(16, 16, 512), (64, 16, 512)],
        [smem()] * 5 + [anywhere()] * 4,
        [vmem(), vmem()],
        [
            VMEM((32, 16, 512), BF),
            VMEM((3, 8, 1024), F32),
            VMEM((3, 8, 1024), F32),
            VMEM((8, 1024), F32),
            VMEM((64, 16, 512), BF),
            VMEM((8, 8, 1024), F32),
            VMEM((512, 1024), BF),
            VMEM((512, 1024), BF),
            VMEM((8, 512, 512), BF),
            VMEM((8, 128, 512), BF),
            VMEM((8, 128, 512), BF),
            VMEM((8, 8, 16, 512), BF),
            VMEM((NC, 16, 16, 512), BF),
            VMEM((1, 640), F32),
            VMEM((NW, 1, 640), F32),
            VMEM((NC + 1, 128, 128), F32),
            VMEM((NC, NW, 16, 128), BF),
            VMEM((1024, 4096), BF),
            VMEM((NC, 1024, 1024), BF),
            VMEM((1024, 1024), BF),
            VMEM((1024, 128), F32),
            VMEM((1024, 128), F32),
            VMEM((1024, 256), BF),
            VMEM((1024, 128), BF),
            VMEM((NC, NW, 16, 128), BF),
            VMEM((NC, 16, 16, 512), BF),
            VMEM((NC, 2, 8, 16, 512), BF),
            VMEM((8, 128, 512), BF),
            VMEM((8, 128, 512), BF),
            dma((8,)),
            dma((NC,)),
            dma((NC,)),
            dma((NC,)),
            dma((NC,)),
            dma((NC,)),
            dma((3,)),
            dma((4,)),
        ],
        0,
    )(
        pair_fine,
        pair_owner.reshape(64),
        pair_coarse,
        coarse_faces.T,
        coarse_inv_mass,
        fine_field_in,
        jnp.transpose(fine_points, (1, 0, 2)),
        jnp.transpose(coarse_points, (1, 0, 2)),
        quad_weights,
    )
    return call(
        finish_kernel,
        [(16, 16, 512), (32, 16, 512)],
        [smem(), smem(), vmem(), vmem()],
        [vmem(), vmem()],
        [VMEM((32, 16, 512), F32)],
    )(pair_fine, fine_inv_mass, terms, coarse)


def solution(mesh):
    placed = (
        P("wide", "field", None),
        P(("wide", "field"), None, None),
        P(("wide", "field"), None, None),
        P(("wide", "field"), None),
        P("wide"),
        P("wide", None),
        P("wide"),
        P("wide", None),
        P("wide"),
        P("wide"),
    )
    return jax.shard_map(
        shards,
        mesh=mesh,
        in_specs=placed,
        out_specs=(P("wide", "field", None), P("wide", "field", None)),
        check_vma=False,
    )
```

```python
import math

import jax
import jax.numpy as jnp
from jax import lax
from jax.experimental import pallas as pl
from jax.experimental.pallas import tpu as pltpu
from jax.sharding import PartitionSpec as P

NB = 8
DIFFUSE = 0.125
MESH = pl.DeviceIdType.MESH
BF = jnp.bfloat16
F32 = jnp.float32
VMEM = pltpu.VMEM
LIMIT = 60 << 20

NY = 8
NW = 64
NF = 8
NC = 4


def peer(wide, k):
    z, y = lax.div(wide, NY), lax.rem(wide, NY)
    return lax.rem(z + k % NY, NW // NY) * NY + lax.rem(y + k % NY + k // NY, NY)


def iota(shape, dim):
    return lax.broadcasted_iota(jnp.int32, shape, dim)


def swap_matrix(rows, minor_out, minor_in):
    r, c = iota((rows, rows), 0), iota((rows, rows), 1)
    return (c == (r % minor_out) * minor_in + r // minor_out).astype(BF)


def dot(a, b, dims=((1,), (0,))):
    return lax.dot_general(a, b, (dims, ((), ())), preferred_element_type=F32)


def legendre_rows(x):
    scale = [math.sqrt((2 * n + 1) / 2.0) for n in range(NB)]
    rows = [jnp.full_like(x, scale[0]), x * scale[1]]
    for n in range(1, NB - 1):
        up = (2 * n + 1) / (n + 1) * scale[n + 1] / scale[n]
        down = n / (n + 1) * scale[n + 1] / scale[n - 1]
        rows.append(up * (x * rows[n]) - down * rows[n - 1])
    return rows


def basis_block(points, at, weight, out_ref, i, lanes):
    def row(d):
        return jnp.broadcast_to(points[i, d : d + 1, lanes], (NB, 128))

    first, second, third = (legendre_rows(row(at + d)) for d in range(3))
    sub = iota((NB, 128), 0)
    minor = third[0]
    for n in range(1, NB):
        minor = jnp.where(sub == n, third[n], minor)
    if weight is not None:
        minor = minor * row(weight)
    pairs = [second[b] * minor for b in range(NB)]
    for a in range(NB):
        block = jnp.concatenate([first[a] * pairs[b] for b in range(NB)], axis=0)
        out_ref[a * 64 : (a + 1) * 64, lanes] = block.astype(BF)


def remap_kernel(
    pair_fine_ref,
    owner_ref,
    pair_coarse_ref,
    coarse_faces_ref,
    coarse_inverse_ref,
    fine_hbm,
    fine_pts_hbm,
    coarse_pts_hbm,
    weights_hbm,
    coarse_ref,
    terms_ref,
    fine_ref,
    fine_pts_ref,
    coarse_pts_ref,
    weights_ref,
    picked,
    points,
    left,
    right,
    tiles,
    rows,
    contrib,
    blocks,
    mixed,
    meta,
    metas,
    stage,
    arrived,
    hot,
    pick,
    faces,
    inverse,
    load,
    solved,
    smooth,
    reply,
    back,
    spread,
    rows_back,
    result,
    send_sem,
    rows_sem,
    blocks_sem,
    arrived_sem,
    back_sem,
    rows_back_sem,
    other_sem,
    input_sem,
):
    wide, field = lax.axis_index("wide"), lax.axis_index("field")
    barrier = pltpu.get_barrier_semaphore()

    for k in range(1, NF):
        pl.semaphore_signal(
            barrier, inc=1, device_id=(wide, lax.rem(field + k, NF)), device_id_type=MESH
        )
    for k in range(1, NW):
        pl.semaphore_signal(
            barrier, inc=1, device_id=(peer(wide, k), field), device_id_type=MESH
        )
    inputs = [
        pltpu.make_async_copy(src, dst, input_sem.at[n])
        for n, (src, dst) in enumerate(
            (
                (fine_hbm, fine_ref),
                (coarse_pts_hbm, coarse_pts_ref),
                (fine_pts_hbm, fine_pts_ref),
                (weights_hbm, weights_ref),
            )
        )
    ]
    for copy in inputs:
        copy.start()

    def wait(ref, sem):
        pltpu.make_async_copy(ref, ref, sem).wait()

    def across(index, src, dst, sem):
        for k in range(1, NW):
            to = peer(wide, k)
            pltpu.make_async_remote_copy(
                src(to), dst, send_sem.at[index], sem, device_id=(to, field), device_id_type=MESH
            ).start()
        pltpu.make_async_copy(src(wide), dst, sem).start()

    def along(index, src, dst, sem):
        for k in range(1, NF):
            to = lax.rem(field + k, NF)
            pltpu.make_async_remote_copy(
                src(to), dst, send_sem.at[index], sem, device_id=(wide, to), device_id_type=MESH
            ).start()
        pltpu.make_async_copy(src(field), dst, sem).start()

    def two(c):
        return pl.ds(2 * c, 2)

    def mine(width):
        return pl.ds(pl.multiple_of(field * width, width), width)

    def block_of(to):
        return pl.ds(pl.multiple_of(to * 16, 16), 16)

    def lanes_of(to):
        return pl.ds(pl.multiple_of(lax.rem(to, 4) * 128, 128), 128)

    def pick_rows(p, carry):
        picked[p] = fine_ref[pair_fine_ref[p]]
        return carry

    inputs[0].wait()
    lax.fori_loop(0, 64, pick_rows, 0, unroll=8)
    pl.semaphore_wait(barrier, NW + NF - 2)

    def send_rows(*pairs):
        for i in pairs:
            along(
                0,
                lambda to: picked.at[to * 8 + i],
                rows.at[i, mine(16), :],
                rows_sem.at[i],
            )

    send_rows(0, 1, 2)

    lane = iota((1, 128), 1)
    for c in range(NC):
        ids = jnp.zeros((1, 128), F32)
        for r in range(16):
            p = (r % 8) * 8 + 2 * c + r // 8
            number = (owner_ref[p] * 16 + pair_coarse_ref[p]).astype(F32)
            ids = jnp.where(lane % 16 == r, number, ids)
        meta[:, c * 128 : (c + 1) * 128] = ids
    values = jnp.zeros((1, 128), F32)
    for e in range(16):
        for face in range(6):
            number = coarse_faces_ref[face, e].astype(F32)
            values = jnp.where(lane == face * 16 + e, number, values)
        values = jnp.where(lane == 96 + e, coarse_inverse_ref[e], values)
    meta[:, 512:640] = values
    across(3, lambda to: meta, metas.at[wide], other_sem.at[0])

    for copy in inputs[1:]:
        copy.wait()
    for i in range(8):
        for d in range(3):
            points[i, d : d + 1, :] = coarse_pts_ref[d, i : i + 1, :]
            points[i, 3 + d : 4 + d, :] = fine_pts_ref[d, i : i + 1, :]
        points[i, 6:7, :] = weights_ref[i : i + 1, :]

    def build(i, carry):
        def chunk(l, c):
            lanes = pl.ds(pl.multiple_of(l * 128, 128), 128)
            basis_block(points, 0, 6, left, i, lanes)
            basis_block(points, 3, None, right, i, lanes)
            return c

        lax.fori_loop(0, 8, chunk, 0)
        tiles[i] = dot(left[...], right[...], ((1,), (1,))).astype(BF)
        return carry

    swap = swap_matrix(256, 16, 16)

    def contribute(*pairs):
        for i in pairs:
            wait(rows.at[i], rows_sem.at[i])
            contrib[i] = dot(rows[i], tiles[i], ((1,), (1,))).astype(BF)
            along(
                1,
                lambda to: contrib.at[i, block_of(to), :],
                blocks.at[i, field],
                blocks_sem.at[i // 2],
            )

    def transpose(c):
        wait(blocks.at[two(c)], blocks_sem.at[c])
        mixed[c] = dot(swap, blocks[two(c)].reshape(256, 512)).astype(BF).reshape(16, 16, 512)
        across(
            2,
            lambda to: mixed.at[c, lax.div(to, 4), :, lanes_of(to)],
            arrived.at[c, wide],
            arrived_sem.at[c],
        )

    lax.fori_loop(0, 2, build, 0)
    contribute(0, 1)
    send_rows(3, 4, 5)
    lax.fori_loop(2, 4, build, 0)
    contribute(2, 3)
    send_rows(6, 7)
    transpose(0)
    lax.fori_loop(4, 6, build, 0)
    contribute(4, 5)
    transpose(1)
    lax.fori_loop(6, 8, build, 0)
    contribute(6, 7)
    transpose(2)
    transpose(3)

    wait(metas, other_sem.at[0])
    stage[...] = jnp.zeros_like(stage)
    for s in range(NW):
        for c in range(NC + 1):
            stage[c, s : s + 1, :] = metas[s, :, c * 128 : (c + 1) * 128]
    element = iota((1024, 128), 0).astype(F32)
    own_lanes = iota((8, 128), 1) // 16 == iota((8, 128), 0)
    for c in range(NC):

        def build_hot(k, carry):
            eight = stage[c, pl.ds(pl.multiple_of(8 * k, 8), 8), :]
            ids = jnp.sum(jnp.where(own_lanes, eight, 0.0), axis=0, keepdims=True)
            at = pl.ds(pl.multiple_of(c * 1024 + k * 128, 128), 128)
            hot[:, at] = (element == ids).astype(F32).astype(BF)
            return carry

        lax.fori_loop(0, 8, build_hot, 0)
    for c in range(NC + 1):
        turned = jnp.transpose(stage[c])
        stage[c] = turned
    few = iota((16, 128), 1)
    many = iota((128, 128), 1)
    number = iota((16, 1024), 1).astype(F32)

    def build_rest(s, carry):
        at = pl.ds(pl.multiple_of(s * 16, 16), 16)
        for c in range(NC):
            ids = jnp.sum(jnp.where(few == s, stage[c, 0:16, :], 0.0), axis=1, keepdims=True)
            pick[c, at, :] = (number == ids).astype(F32).astype(BF)
        column = jnp.sum(jnp.where(many == s, stage[NC], 0.0), axis=1, keepdims=True)
        count = jnp.zeros((16, 1024), F32)
        for face in range(6):
            count += (number == column[face * 16 : (face + 1) * 16]).astype(F32)
        faces[at, :] = count.astype(BF)
        inverse[at, :] = jnp.broadcast_to(column[96:112], (16, 128))
        return carry

    lax.fori_loop(0, NW, build_rest, 0)

    for c in range(NC):
        wait(arrived.at[c], arrived_sem.at[c])

        more = dot(hot[:, c * 1024 : (c + 1) * 1024], arrived[c].reshape(1024, 128))
        if c:
            more = load[...] + more
        if c < NC - 1:
            load[...] = more
        else:
            total = more * inverse[...]
            high = total.astype(BF)
            solved[:, 0:128] = high
            solved[:, 128:256] = (total - high.astype(F32)).astype(BF)
            load[...] = total

    def smooth_rows(m, carry):
        at = pl.ds(pl.multiple_of(m * 512, 512), 512)
        both = dot(faces[at, :], solved[...])
        own = load[at, :]
        beside = both[:, 0:128] + both[:, 128:256]
        smooth[at, :] = (own + DIFFUSE * (beside - 6.0 * own)).astype(BF)
        return carry

    lax.fori_loop(0, 2, smooth_rows, 0)

    def answer(c):
        reply[c] = dot(pick[c], smooth[...]).astype(BF).reshape(NW, 16, 128)
        across(
            4,
            lambda to: reply.at[c, to],
            back.at[c, lax.div(wide, 4), :, lanes_of(wide)],
            back_sem.at[c],
        )

    def finish(*pairs):
        for i in pairs:
            wait(rows_back.at[i], rows_back_sem.at[i])
            result[i] = dot(rows_back[i], tiles[i]).astype(BF)
            along(
                7,
                lambda to: result.at[i, block_of(to), :],
                terms_ref.at[field * 8 + i],
                other_sem.at[2],
            )

    answer(0)
    answer(1)
    for c in range(NC):
        wait(back.at[c], back_sem.at[c])
        turned = dot(swap, back[c].reshape(256, 512)).astype(BF)
        spread[c] = turned.reshape(2, 8, 16, 512)
        for i in (2 * c, 2 * c + 1):
            along(
                6,
                lambda to: spread.at[c, i % 2, to],
                rows_back.at[i, mine(16), :],
                rows_back_sem.at[i],
            )
        if c + 2 < NC:
            answer(c + 2)
        elif c + 2 == NC:
            across(
                5,
                lambda to: smooth.at[block_of(to)],
                coarse_ref.at[lax.div(wide, 4), :, lanes_of(wide)],
                other_sem.at[1],
            )
        if c:
            finish(2 * c - 2, 2 * c - 1)
    finish(2 * NC - 2, 2 * NC - 1)
    wait(coarse_ref, other_sem.at[1])
    wait(terms_ref, other_sem.at[2])
    for index in (0, 1, 6, 7):
        wait(picked.at[pl.ds(0, 56)], send_sem.at[index])
    wait(metas.at[pl.ds(0, NW - 1)], send_sem.at[3])
    for index in (2, 4):
        for c in range(NC):
            wait(arrived.at[c, pl.ds(0, NW - 1)], send_sem.at[index])
    wait(arrived.at[0, pl.ds(0, NW - 1)], send_sem.at[5])


def finish_kernel(
    pair_fine_ref, inverse_ref, terms_ref, coarse_ref, coarse_out_ref, fine_out_ref, total, other
):
    swap = swap_matrix(256, 16, 16)
    block = coarse_ref[...].reshape(256, 512)
    coarse_out_ref[...] = dot(swap, block).astype(BF).reshape(16, 16, 512)
    total[...] = jnp.zeros_like(total)
    other[...] = jnp.zeros_like(other)

    def add(p, carry):
        first, second = pair_fine_ref[p], pair_fine_ref[p + 32]
        total[first] += terms_ref[p].astype(F32)
        other[second] += terms_ref[p + 32].astype(F32)
        return carry

    lax.fori_loop(0, 32, add, 0, unroll=4)

    def store(e, carry):
        fine_out_ref[e] = (inverse_ref[e] * (total[e] + other[e])).astype(BF)
        return carry

    lax.fori_loop(0, 32, store, 0, unroll=4)


def vmem():
    return pl.BlockSpec(memory_space=pltpu.VMEM)


def smem():
    return pl.BlockSpec(memory_space=pltpu.SMEM)


def anywhere():
    return pl.BlockSpec(memory_space=pl.ANY)


def call(kernel, outs, in_specs, out_specs, scratch, number=None, cost=None):
    params = {"vmem_limit_bytes": LIMIT}
    if number is not None:
        params.update(collective_id=number, has_side_effects=True)
    return pl.pallas_call(
        kernel,
        out_shape=[jax.ShapeDtypeStruct(shape, BF) for shape in outs],
        in_specs=in_specs,
        out_specs=out_specs,
        scratch_shapes=scratch,
        compiler_params=pltpu.CompilerParams(**params),
    )


def shards(
    fine_field_in,
    fine_points,
    coarse_points,
    quad_weights,
    pair_fine,
    pair_owner,
    pair_coarse,
    coarse_faces,
    coarse_inv_mass,
    fine_inv_mass,
):
    dma = pltpu.SemaphoreType.DMA
    coarse, terms = call(
        remap_kernel,
        [(16, 16, 512), (64, 16, 512)],
        [smem()] * 5 + [anywhere()] * 4,
        [vmem(), vmem()],
        [
            VMEM((32, 16, 512), BF),
            VMEM((3, 8, 1024), F32),
            VMEM((3, 8, 1024), F32),
            VMEM((8, 1024), F32),
            VMEM((64, 16, 512), BF),
            VMEM((8, 8, 1024), F32),
            VMEM((512, 1024), BF),
            VMEM((512, 1024), BF),
            VMEM((8, 512, 512), BF),
            VMEM((8, 128, 512), BF),
            VMEM((8, 128, 512), BF),
            VMEM((8, 8, 16, 512), BF),
            VMEM((NC, 16, 16, 512), BF),
            VMEM((1, 640), F32),
            VMEM((NW, 1, 640), F32),
            VMEM((NC + 1, 128, 128), F32),
            VMEM((NC, NW, 16, 128), BF),
            VMEM((1024, 4096), BF),
            VMEM((NC, 1024, 1024), BF),
            VMEM((1024, 1024), BF),
            VMEM((1024, 128), F32),
            VMEM((1024, 128), F32),
            VMEM((1024, 256), BF),
            VMEM((1024, 128), BF),
            VMEM((NC, NW, 16, 128), BF),
            VMEM((NC, 16, 16, 512), BF),
            VMEM((NC, 2, 8, 16, 512), BF),
            VMEM((8, 128, 512), BF),
            VMEM((8, 128, 512), BF),
            dma((8,)),
            dma((8,)),
            dma((NC,)),
            dma((NC,)),
            dma((NC,)),
            dma((8,)),
            dma((3,)),
            dma((4,)),
        ],
        0,
    )(
        pair_fine,
        pair_owner.reshape(64),
        pair_coarse,
        coarse_faces.T,
        coarse_inv_mass,
        fine_field_in,
        jnp.transpose(fine_points, (1, 0, 2)),
        jnp.transpose(coarse_points, (1, 0, 2)),
        quad_weights,
    )
    return call(
        finish_kernel,
        [(16, 16, 512), (32, 16, 512)],
        [smem(), smem(), vmem(), vmem()],
        [vmem(), vmem()],
        [VMEM((32, 16, 512), F32), VMEM((32, 16, 512), F32)],
    )(pair_fine, fine_inv_mass, terms, coarse)


def solution(mesh):
    placed = (
        P("wide", "field", None),
        P(("wide", "field"), None, None),
        P(("wide", "field"), None, None),
        P(("wide", "field"), None),
        P("wide"),
        P("wide", None),
        P("wide"),
        P("wide", None),
        P("wide"),
        P("wide"),
    )
    return jax.shard_map(
        shards,
        mesh=mesh,
        in_specs=placed,
        out_specs=(P("wide", "field", None), P("wide", "field", None)),
        check_vma=False,
    )
```
